32 devices in a mesh: dp: 4 (over z), seq: 2 (over y), tensor: 4 (over x, core).
Axes of the slice: x: 2, y: 2, z: 4, core: 2. Of those that a mesh axis runs over, the one named last changes fastest.
Arguments:
- activations: bfloat16 [2048, 512], P(('dp', 'seq')), may hold values from -6 to 6
- d_logits: bfloat16 [2048, 2048], P(('dp', 'seq'), 'tensor'), may hold values from -0.0234375 to 0.0234375
- block_owner: int32 [4], replicated, may hold values from 0 to 3, each once
- left_stat: float32 [4, 512, 512], P('dp', ('seq', 'tensor')), may hold values from -0.1 to 2.1
- right_stat: float32 [4, 512, 512], P('dp', ('seq', 'tensor')), may hold values from -0.1 to 2.1
- second_moment: float32 [4, 512, 512], P('dp', ('seq', 'tensor')), may hold values from 2e-05 to 0.002
- left_root: float32 [4, 512, 512], P('dp', ('seq', 'tensor')), may hold values from -0.15 to 14
- right_root: float32 [4, 512, 512], P('dp', ('seq', 'tensor')), may hold values from -0.15 to 14
Outputs:
- update: bfloat16 [4, 512, 512], P(None, ('seq', 'tensor'))
- left_new: float32 [4, 512, 512], P('dp', ('seq', 'tensor'))
- right_new: float32 [4, 512, 512], P('dp', ('seq', 'tensor'))
- moment_new: float32 [4, 512, 512], P('dp', ('seq', 'tensor'))
The draws below stay inside these ranges and needn't reach their ends.
All inputs are finite; a program needn't handle non-finite values.
Results may differ from the reference program's by a relative error of at most 0.00055.
Values may be sent and summed in bfloat16 or wider, within the bound.
No kernel may reach another device: no remote copies, remote signals or barrier semaphores. Data moves between devices by JAX's collectives and lax.ppermute only.
A program may use at most 64 MiB of HBM per device.

```python
import math
import jax
import jax.numpy as jnp
from jax import lax

BLK = 512
TOKENS = 2048
NBLK = 4
VW = 2048
BR = 128
RS = 64
N_SEQ = 2
N_TENSOR = 4


def symmetric_blocks(key, diag_lo, diag_hi, spread, rise):
    key_diag, key_off = jax.random.split(key)
    position = jnp.arange(BLK, dtype=jnp.float32) / BLK
    slope = math.log(rise)
    noise = jax.random.truncated_normal(key_off, -4.0, 4.0, (NBLK, BLK, BLK), jnp.float32)
    diagonal = jnp.exp(jax.random.uniform(key_diag, (NBLK, BLK), jnp.float32, math.log(diag_lo), math.log(diag_hi)))
    diagonal = diagonal * jnp.exp(slope * position)[None, :]
    symmetric = 0.5 * spread * (noise + jnp.swapaxes(noise, 1, 2))
    return symmetric + diagonal[:, :, None] * jnp.eye(BLK, dtype=jnp.float32)[None, :, :]


def draw_left_stat(key, part):
    return symmetric_blocks(jax.random.fold_in(key, 101), 0.5, 2.0, 0.02, 1.0)


def draw_right_stat(key, part):
    return symmetric_blocks(jax.random.fold_in(key, 102), 0.5, 2.0, 0.02, 1.0)


def draw_left_root(key, part):
    return symmetric_blocks(jax.random.fold_in(key, 103), 0.5, 1.5, 0.03, 3.0)


def draw_right_root(key, part):
    return symmetric_blocks(jax.random.fold_in(key, 104), 0.5, 1.5, 0.03, 3.0)


def draw_second_moment(key, part):
    folded = jax.random.fold_in(key, 105)
    position = jnp.arange(BLK, dtype=jnp.float32) / BLK
    falling = jnp.exp(-math.log(9.0) * position)[None, :, None]
    base_value = jnp.exp(jax.random.uniform(folded, (NBLK, BLK, BLK), jnp.float32, math.log(0.0002), math.log(0.002)))
    return base_value * falling


def raised(result, stream_key, source, target, parts, factor):
    owner, partner = [(jnp.arange(result.shape[axis_at]) // (result.shape[axis_at] // parts)).reshape([-1 if axis == axis_at else 1 for axis in range(result.ndim)]) for axis_at in (source, target)]
    chosen = jax.random.permutation(stream_key, parts)[partner]
    strong = (owner == chosen) | (owner == (partner + parts // 2) % parts)
    return jnp.where(strong, factor * result, result)


def levels(rng, shape, cuts, least, top_value):
    def one(dim, shards_of):
        steps = jax.random.uniform(jax.random.fold_in(jax.random.fold_in(rng, 6), dim), (shards_of,), jnp.float32, least / len(cuts), top_value / len(cuts))
        return jnp.repeat(jnp.exp(steps), shape[dim] // shards_of).reshape((-1,) + (1,) * (len(shape) - dim - 1))

    level = one(*cuts[0])
    for cut in cuts[1:]:
        level = level * one(*cut)
    return level


def bell_draw(own_key, dims, width, bound, shards=(), kind=jnp.bfloat16):
    values = jax.random.normal(own_key, dims, jnp.float32) * width
    if len(shards) > 0:
        values = levels(own_key, dims, shards, -0.22, 0.18) * values
    return jnp.clip(values, min=-bound, max=bound).astype(kind)


def bell_draw_with(own_key, shape, deviation, bound, cuts, heavy, held_as=jnp.bfloat16):
    result = deviation * jax.random.normal(own_key, shape, jnp.float32)
    if cuts:
        result = result * levels(own_key, shape, cuts, -0.22, 0.18)
    return jnp.clip(raised(result, jax.random.fold_in(own_key, 3), *heavy), -bound, bound).astype(held_as)


def setup_inputs(seed: int = 0) -> dict:
    keys = jax.random.split(jax.random.key(seed), 9)
    return {
        "activations": bell_draw(keys[0], (TOKENS, BLK), 1.0, 6.0, ((0, 8),)),
        "d_logits": bell_draw_with(keys[1], (TOKENS, VW), (0.05 * TOKENS ** -0.5), 0.0234375, ((0, 8), (1, 4)), (0, 1, 8, 2.0)),
        "block_owner": jax.random.permutation(keys[2], NBLK).astype(jnp.int32),
        "left_stat": draw_left_stat(jax.random.fold_in(keys[8], 71), 0),
        "right_stat": draw_right_stat(jax.random.fold_in(keys[8], 71), 0),
        "second_moment": draw_second_moment(jax.random.fold_in(keys[8], 71), 0),
        "left_root": draw_left_root(jax.random.fold_in(keys[8], 71), 0),
        "right_root": draw_right_root(jax.random.fold_in(keys[8], 71), 0),
    }


highest = lax.Precision.HIGHEST

def reference(activations, d_logits, block_owner, left_stat, right_stat, second_moment, left_root, right_root):
    gradient = lax.dot_general(d_logits, activations, (((0,), (0,)), ((), ())), preferred_element_type=jnp.float32)
    blocks = gradient.reshape(N_TENSOR, NBLK, BR, BLK).reshape(N_TENSOR, NBLK, N_SEQ, RS, BLK)
    blocks = blocks.transpose(1, 2, 0, 3, 4).reshape(NBLK, BLK, BLK)
    owner_block = jnp.zeros((NBLK,), jnp.int32).at[block_owner].set(jnp.arange(NBLK, dtype=jnp.int32))
    owned_blocks = blocks[owner_block]

    def per_owner(operands):
        grad_block, left_old, right_old, moment_old, left_factor, right_factor = operands
        left_next = 0.95 * left_old + jnp.dot(grad_block, grad_block.T, precision=highest, preferred_element_type=jnp.float32)
        right_next = 0.95 * right_old + jnp.dot(grad_block.T, grad_block, precision=highest, preferred_element_type=jnp.float32)
        moment_next = 0.99 * moment_old + 0.01 * grad_block * grad_block
        adam_dir = grad_block / (jnp.sqrt(moment_next) + 1e-08)
        mixed_rows = jnp.dot(left_factor, grad_block, precision=highest, preferred_element_type=jnp.float32)
        precond = jnp.dot(mixed_rows, right_factor, precision=highest, preferred_element_type=jnp.float32)
        graft_scale = jnp.sqrt(jnp.sum(adam_dir * adam_dir)) / (jnp.sqrt(jnp.sum(precond * precond)) + 1e-06)
        return ((graft_scale * precond).astype(jnp.bfloat16), left_next, right_next, moment_next)
    updates, left_new, right_new, moment_new = lax.map(per_owner, (owned_blocks, left_stat, right_stat, second_moment, left_root, right_root))
    update = updates[block_owner]
    return (update, left_new, right_new, moment_new)
```

```python
import jax
import jax.numpy as jnp
from jax import lax
from jax.sharding import PartitionSpec as P


highest = lax.Precision.HIGHEST
AXES = ("dp", "seq", "tensor")


def swap(sizes, value, dp=0, seq=0, tensor=0):
    owners, seqs, tensors = sizes
    pairs = []
    for d in range(owners):
        for s in range(seqs):
            for t in range(tensors):
                here = (d * seqs + s) * tensors + t
                there = ((d ^ dp) * seqs + (s ^ seq)) * tensors + (t ^ tensor)
                pairs.append((here, there))
    return lax.ppermute(value, AXES, pairs)


def rows_at(value, start, count):
    return lax.dynamic_slice_in_dim(value, start, count, 0)


def gather_rows(sizes, value, rank, width):
    _, seqs, tensors = sizes
    full = jnp.zeros((seqs * tensors,) + value.shape, value.dtype)
    steps = [(s, t) for s in range(seqs) for t in range(0, tensors, 2)]
    mine = [value] + [swap(sizes, value, seq=s, tensor=t) for s, t in steps[1:]]
    other = swap(sizes, jnp.stack(mine), tensor=1)
    for index, (s, t) in enumerate(steps):
        place = rank ^ (s * tensors + t)
        full = lax.dynamic_update_slice_in_dim(full, mine[index][None], place, 0)
        full = lax.dynamic_update_slice_in_dim(full, other[index][None], place ^ 1, 0)
    return full


def per_device(
    sizes, activations, d_logits, block_owner, left_stat, right_stat, second_moment, left_root, right_root
):
    owners, seqs, tensors = sizes
    tokens_here = d_logits.shape[0]
    half = tokens_here // 2
    width = activations.shape[1]
    share = width // (seqs * tensors)
    band = width // tensors
    d, s, t = (lax.axis_index(name) for name in AXES)
    parity = t & 1
    rank = s * tensors + t

    def columns_of(owner):
        picked = jnp.zeros((tokens_here, band), d_logits.dtype)
        for b in range(owners):
            own = d_logits[:, b * band : (b + 1) * band]
            picked = jnp.where(block_owner[b] == owner, own, picked)
        return picked

    near = rows_at(activations, parity * half, half)
    far = rows_at(activations, (1 - parity) * half, half)

    def package(owner):
        picked = columns_of(owner)
        return jnp.concatenate(
            [near, rows_at(picked, parity * half, half), rows_at(picked, (1 - parity) * half, half)], axis=1
        )

    arrived = [swap(sizes, package(d ^ k), dp=k) for k in range(1, owners)]
    roots = gather_rows(sizes, jnp.concatenate([left_root[0], right_root[0]], axis=0), rank, width)
    left_full = roots[:, :share].reshape(width, width)
    right_full = roots[:, share:].reshape(width, width)

    near_rows = jnp.concatenate([p[:, :width] for p in arrived], axis=0)
    far_rows = swap(sizes, near_rows, tensor=1)
    own = columns_of(d)
    left_hand = jnp.concatenate(
        [own]
        + [p[:, width : width + band] for p in arrived]
        + [p[:, width + band :] for p in arrived],
        axis=0,
    )
    right_hand = jnp.concatenate([activations, near_rows, far_rows], axis=0)
    partial = lax.dot_general(
        left_hand, right_hand, (((0,), (0,)), ((), ())), preferred_element_type=jnp.float32
    )
    slab = rows_at(partial, s * share, share)
    for k in range(1, seqs):
        slab = slab + swap(sizes, rows_at(partial, (s ^ k) * share, share), seq=k)

    moment_next = 0.99 * second_moment[0] + 0.01 * slab * slab
    adam_dir = slab / (jnp.sqrt(moment_next) + 1e-08)
    adam_part = jnp.sum(adam_dir * adam_dir)
    carried = jnp.concatenate([slab, jnp.full((8, width), adam_part, jnp.float32)], axis=0)
    gathered = gather_rows(sizes, carried, rank, width)
    grad = gathered[:, :share].reshape(width, width)
    adam_total = jnp.sum(gathered[:, share, 0])

    mixed = jnp.dot(left_full, grad, precision=highest, preferred_element_type=jnp.float32)
    precond = jnp.dot(mixed, right_full, precision=highest, preferred_element_type=jnp.float32)
    precond_total = jnp.sum(precond * precond)
    graft_scale = jnp.sqrt(adam_total) / (jnp.sqrt(precond_total) + 1e-06)
    update_rows = (graft_scale * rows_at(precond, rank * share, share)).astype(jnp.bfloat16)
    sent = [update_rows] + [swap(sizes, update_rows, dp=k) for k in range(1, owners)]

    outer_rows = jnp.dot(slab, grad.T, precision=highest, preferred_element_type=jnp.float32)
    own_columns = lax.dynamic_slice_in_dim(grad, rank * share, share, 1)
    right_part = jnp.dot(own_columns.T, grad, precision=highest, preferred_element_type=jnp.float32)
    left_next = 0.95 * left_stat[0] + outer_rows
    right_next = 0.95 * right_stat[0] + right_part

    update = []
    for b in range(owners):
        row = sent[0]
        for k in range(1, owners):
            row = jnp.where((block_owner[b] ^ d) == k, sent[k], row)
        update.append(row)
    return (jnp.stack(update), left_next[None], right_next[None], moment_next[None])


def solution(mesh):
    sizes = tuple(mesh.shape[name] for name in AXES)

    def body(*arrays):
        return per_device(sizes, *arrays)

    return jax.shard_map(
        body,
        mesh=mesh,
        in_specs=(
            P(("dp", "seq"), None),
            P(("dp", "seq"), "tensor"),
            P(),
            P("dp", ("seq", "tensor"), None),
            P("dp", ("seq", "tensor"), None),
            P("dp", ("seq", "tensor"), None),
            P("dp", ("seq", "tensor"), None),
            P("dp", ("seq", "tensor"), None),
        ),
        out_specs=(
            P(None, ("seq", "tensor"), None),
            P("dp", ("seq", "tensor"), None),
            P("dp", ("seq", "tensor"), None),
            P("dp", ("seq", "tensor"), None),
        ),
        check_vma=False,
    )
```

```python
import functools
import jax
import jax.numpy as jnp
from jax import lax
from jax.experimental import pallas as pl
from jax.experimental.pallas import tpu as pltpu
from jax.sharding import PartitionSpec as P


highest = lax.Precision.HIGHEST
AXES = ("dp", "seq", "tensor")
MIB = 1 << 20


def swap(sizes, value, dp=0, seq=0, tensor=0):
    owners, seqs, tensors = sizes
    pairs = []
    for d in range(owners):
        for s in range(seqs):
            for t in range(tensors):
                here = (d * seqs + s) * tensors + t
                there = ((d ^ dp) * seqs + (s ^ seq)) * tensors + (t ^ tensor)
                pairs.append((here, there))
    return lax.ppermute(value, AXES, pairs)


def group_steps(sizes):
    _, seqs, tensors = sizes
    same = [(s, t) for s in range(seqs) for t in range(0, tensors, 2)]
    return [s * tensors + t for s, t in same] + [s * tensors + t + 1 for s, t in same]


def gather_pieces(sizes, value):
    _, seqs, tensors = sizes
    same = [(s, t) for s in range(seqs) for t in range(0, tensors, 2)]
    mine = [value] + [swap(sizes, value, seq=s, tensor=t) for s, t in same[1:]]
    return mine + [swap(sizes, piece, tensor=1) for piece in mine]


def whole():
    return pl.BlockSpec(memory_space=pltpu.VMEM)


def call(body, out, operands, name, scalars=0, scratch=(), limit=16, cost=None):
    in_specs = [pl.BlockSpec(memory_space=pltpu.SMEM)] * scalars + [whole()] * (len(operands) - scalars)
    return pl.pallas_call(
        body,
        out_shape=tuple(jax.ShapeDtypeStruct(shape, dtype) for shape, dtype in out),
        in_specs=in_specs,
        out_specs=tuple(whole() for _ in out),
        scratch_shapes=list(scratch),
        name=name,
        compiler_params=pltpu.CompilerParams(vmem_limit_bytes=limit * MIB),
        cost_estimate=cost,
    )(*operands)


def package_kernel(sizes, owner_ref, act_ref, logit_ref, own_ref, *send_refs):
    owners, _, tensors = sizes
    half = act_ref.shape[0] // 2
    width = act_ref.shape[1]
    band = logit_ref.shape[1] // owners
    d, parity = lax.axis_index("dp"), lax.axis_index("tensor") & 1
    near = pl.ds(pl.multiple_of(parity * half, half), half)
    far = pl.ds(pl.multiple_of((1 - parity) * half, half), half)
    for b in range(owners):
        columns = slice(b * band, (b + 1) * band)
        distance = owner_ref[b] ^ d

        @pl.when(distance == 0)
        def _():
            own_ref[...] = logit_ref[:, columns]

        for k, send_ref in enumerate(send_refs, 1):

            @pl.when(distance == k)
            def _():
                send_ref[:, width : width + band] = logit_ref[near, columns]
                send_ref[:, width + band :] = logit_ref[far, columns]

    for send_ref in send_refs:
        send_ref[:, :width] = act_ref[near, :]


def slab_kernel(kept_ref, came_refs, moment_ref, carry_ref, next_ref):
    share = moment_ref.shape[0]
    rows = pl.ds(pl.multiple_of(lax.axis_index("seq") * share, share), share)
    slab = kept_ref[rows, :]
    for came_ref in came_refs:
        slab = slab + came_ref[...]
    moment_next = 0.99 * moment_ref[...] + 0.01 * slab * slab
    adam_dir = slab / (jnp.sqrt(moment_next) + 1e-08)
    next_ref[...] = moment_next
    carry_ref[:share, :] = slab
    squares = adam_dir * adam_dir
    sums = squares[:8, :]
    for at in range(8, share, 8):
        sums = sums + squares[at : at + 8, :]
    carry_ref[share:, :] = sums


def place_of(sizes, step, share):
    rank = lax.axis_index("seq") * sizes[2] + lax.axis_index("tensor")
    return pl.ds(pl.multiple_of((rank ^ step) * share, share), share)


def roots_kernel(sizes, *refs):
    steps = group_steps(sizes)
    pieces, (left_ref, right_ref) = refs[: len(steps)], refs[len(steps) :]
    share = pieces[0].shape[0] // 2
    for step, piece in zip(steps, pieces):
        rows = place_of(sizes, step, share)
        left_ref[rows, :] = piece[:share, :]
        right_ref[rows, :] = piece[share:, :]


def precond_kernel(sizes, left_ref, right_ref, *refs):
    steps = group_steps(sizes)
    pieces, (update_ref, grad_ref, precond_ref) = refs[: len(steps)], refs[len(steps) :]
    share = update_ref.shape[0]
    adam = None
    for step, piece in zip(steps, pieces):
        grad_ref[place_of(sizes, step, share), :] = piece[:share, :]
    rank = lax.axis_index("seq") * sizes[2] + lax.axis_index("tensor")
    mixed = jnp.dot(left_ref[...], grad_ref[...], precision=highest, preferred_element_type=jnp.float32)
    precond = jnp.dot(mixed, right_ref[...], precision=highest, preferred_element_type=jnp.float32)
    precond_ref[...] = precond
    for piece in pieces:
        part = piece[share:, :]
        adam = part if adam is None else adam + part
    adam_total = jnp.sum(adam, keepdims=True)
    precond_total = jnp.sum(precond * precond, keepdims=True)
    graft_scale = jnp.sqrt(adam_total) / (jnp.sqrt(precond_total) + 1e-06)
    update_ref[...] = (graft_scale * precond_ref[place_of(sizes, 0, share), :]).astype(update_ref.dtype)


def per_device(
    sizes, activations, d_logits, block_owner, left_stat, right_stat, second_moment, left_root, right_root
):
    owners, seqs, tensors = sizes
    half = d_logits.shape[0] // 2
    width = activations.shape[1]
    share = width // (seqs * tensors)
    band = width // tensors
    d, s, t = (lax.axis_index(name) for name in AXES)
    rank = s * tensors + t

    own, *sends = call(
        functools.partial(package_kernel, sizes),
        [((2 * half, band), jnp.bfloat16)] + [((half, width + 2 * band), jnp.bfloat16)] * (owners - 1),
        (block_owner, activations, d_logits),
        "package",
        scalars=1,
    )
    arrived = []
    for k, send in enumerate(sends, 1):
        with jax.named_scope(f"cross_{k}"):
            arrived.append(swap(sizes, send, dp=k))
    with jax.named_scope("roots"):
        root_pieces = gather_pieces(sizes, jnp.concatenate([left_root[0], right_root[0]], axis=0))
        left_full, right_full = call(
            functools.partial(roots_kernel, sizes), [((width, width), jnp.float32)] * 2, root_pieces, "roots"
        )

    far_rows = [swap(sizes, p[:, :width], tensor=1) for p in arrived]
    left_hand = jnp.concatenate(
        [own]
        + [p[:, width : width + band] for p in arrived]
        + [p[:, width + band :] for p in arrived],
        axis=0,
    )
    right_hand = jnp.concatenate([activations] + [p[:, :width] for p in arrived] + far_rows, axis=0)
    partial = lax.dot_general(
        left_hand, right_hand, (((0,), (0,)), ((), ())), preferred_element_type=jnp.float32
    )
    came = [
        swap(sizes, lax.dynamic_slice_in_dim(partial, (s ^ k) * share, share, 0), seq=k)
        for k in range(1, seqs)
    ]

    def slab_body(kept_ref, *refs):
        slab_kernel(kept_ref, refs[: seqs - 1], *refs[seqs - 1 :])

    carry, moment_next = call(
        slab_body,
        [((share + 8, width), jnp.float32), ((share, width), jnp.float32)],
        (partial, *came, second_moment[0]),
        "slab",
    )
    pieces = gather_pieces(sizes, carry)
    update_rows, grad = call(
        functools.partial(precond_kernel, sizes),
        [((share, width), jnp.bfloat16), ((width, width), jnp.float32)],
        (left_full, right_full, *pieces),
        "precond",
        scratch=[pltpu.VMEM((width, width), jnp.float32)],
        limit=24,
    )
    sent = [update_rows] + [swap(sizes, update_rows, dp=k) for k in range(1, owners)]

    slab = carry[:share]
    outer_rows = jnp.dot(slab, grad.T, precision=highest, preferred_element_type=jnp.float32)
    own_columns = lax.dynamic_slice_in_dim(grad, rank * share, share, 1)
    right_part = jnp.dot(own_columns.T, grad, precision=highest, preferred_element_type=jnp.float32)
    left_next = 0.95 * left_stat[0] + outer_rows
    right_next = 0.95 * right_stat[0] + right_part

    distance = (block_owner ^ d)[:, None, None]
    update = jnp.broadcast_to(sent[0][None], (owners,) + sent[0].shape)
    for k in range(1, owners):
        update = jnp.where(distance == k, sent[k][None], update)
    return (update, left_next[None], right_next[None], moment_next[None])


def solution(mesh):
    sizes = tuple(mesh.shape[name] for name in AXES)

    def body(*arrays):
        return per_device(sizes, *arrays)

    return jax.shard_map(
        body,
        mesh=mesh,
        in_specs=(
            P(("dp", "seq"), None),
            P(("dp", "seq"), "tensor"),
            P(),
            P("dp", ("seq", "tensor"), None),
            P("dp", ("seq", "tensor"), None),
            P("dp", ("seq", "tensor"), None),
            P("dp", ("seq", "tensor"), None),
            P("dp", ("seq", "tensor"), None),
        ),
        out_specs=(
            P(None, ("seq", "tensor"), None),
            P("dp", ("seq", "tensor"), None),
            P("dp", ("seq", "tensor"), None),
            P("dp", ("seq", "tensor"), None),
        ),
        check_vma=False,
    )
```
